32 devices in a mesh: view: 2 (over y), tile: 4 (over z), slab: 4 (over x, core).
Axes of the slice: x: 2, y: 2, z: 4, core: 2. Of those that a mesh axis runs over, the one named last changes fastest.
Arguments:
- estimate: float32 [64, 64, 128], P('slab', 'tile'), may hold values from 0.5 to 2
- recorded: float32 [2, 64, 64, 128], P('view', 'slab', 'tile'), may hold values from 0.25 to 4
- x_index: int32 [2, 64, 128], P('view', 'slab'), may hold values from 0 to 15
- y_index: int32 [2, 64, 64], P('view', 'slab', 'tile'), may hold values from 0 to 15
- z_index: int32 [2, 64, 128], P('view', 'tile'), may hold values from 0 to 15
- profiles: float32 [2, 3, 16, 31], P('view'), may hold values from 0.01 to 1
Outputs:
- updated: float32 [64, 64, 128], P('slab', 'tile')
The draws below stay inside these ranges and needn't reach their ends.
All inputs are finite; a program needn't handle non-finite values.
Results may differ from the reference program's by a relative error of at most 0.00005.
Values sent between devices are 32-bit elements; how exact they have to be, the bound alone decides.
A program may use at most 64 MiB of HBM per device.

```python
import math
import jax
import jax.numpy as jnp
from jax import lax

NY = 128
TAPS = 31
NPROF = 16
VIEWS = 2
NX = 64
NZ = 64


def with_ends(array, own_key, smallest, top_value):
    index_at = [jax.random.randint(jax.random.fold_in(own_key, axis), (), 0, length) for axis, length in enumerate(array.shape)]
    longest = array.shape.index(max(array.shape))
    next_to = index_at[:longest] + [(index_at[longest] + 1) % array.shape[longest]] + index_at[longest + 1:]
    return array.at[tuple(index_at)].set(smallest).at[tuple(next_to)].set(top_value)


def levels(stream_key, shape, cuts, least, largest):
    gain, own = 1.0, jax.random.fold_in(stream_key, 6)
    for axis_at, shards_of in cuts:
        steps = jnp.exp(jax.random.uniform(jax.random.fold_in(own, axis_at), (shards_of,), jnp.float32, least / len(cuts), largest / len(cuts)))
        gain = gain * jnp.repeat(steps, shape[axis_at] // shards_of).reshape([-1 if axis == axis_at else 1 for axis in range(len(shape))])
    return gain


def setup_inputs(seed: int = 0) -> dict:
    keys = jax.random.split(jax.random.key(seed), 7)
    return {
        "estimate": jnp.clip(jnp.exp(math.log(2.0) - 1.3862944 * jax.random.uniform(keys[0], (NZ, NX, NY), jnp.float32) ** levels(keys[0], (NZ, NX, NY), ((0, 4), (1, 4)), -0.2, 0.2)), 0.5, 2.0),
        "recorded": jnp.clip(jnp.exp(math.log(4.0) - 2.7725887 * jax.random.uniform(keys[1], (VIEWS, NZ, NX, NY), jnp.float32) ** levels(keys[1], (VIEWS, NZ, NX, NY), ((0, 2), (1, 4), (2, 4)), -0.2, 0.2)), 0.25, 4.0),
        "x_index": with_ends(jax.random.randint(keys[2], (VIEWS, NZ, NY), 0, NPROF), jax.random.fold_in(keys[2], 1), 0, NPROF - 1).astype(jnp.int32),
        "y_index": with_ends(jax.random.randint(keys[3], (VIEWS, NZ, NX), 0, NPROF), jax.random.fold_in(keys[3], 1), 0, NPROF - 1).astype(jnp.int32),
        "z_index": with_ends(jax.random.randint(keys[4], (VIEWS, NX, NY), 0, NPROF), jax.random.fold_in(keys[4], 1), 0, NPROF - 1).astype(jnp.int32),
        "profiles": jnp.clip(jnp.exp(math.log(1.0) - 4.6051702 * jax.random.uniform(keys[5], (VIEWS, 3, NPROF, TAPS), jnp.float32) ** levels(keys[5], (VIEWS, 3, NPROF, TAPS), ((0, 2),), -0.2, 0.2)), 0.01, 1.0),
    }


def banded(padded, weights, dim, adjoint):
    count = padded.shape[dim] - 30
    total = None
    for k in range(31):
        start = 30 - k if adjoint else k
        term = weights[..., k] * lax.slice_in_dim(padded, start, start + count, axis=dim)
        total = term if total is None else total + term
    return total


def pad_along(field, dim):
    widths = [(0, 0)] * field.ndim
    widths[dim] = (15, 15)
    return jnp.pad(field, widths)


def reference(estimate, recorded, x_index, y_index, z_index, profiles):
    weights = profiles / jnp.sum(profiles, axis=-1, keepdims=True)

    def one_view(total, items):
        data, xi, yi, zi, table = items
        x_taps = jnp.take(table[0], xi, axis=0)[:, None, :, :]
        y_taps = jnp.take(table[1], yi, axis=0)[:, :, None, :]
        z_taps = jnp.take(table[2], zi, axis=0)[None, :, :, :]
        along_x = banded(pad_along(estimate, 1), x_taps, 1, False)
        along_y = banded(pad_along(along_x, 2), y_taps, 2, False)
        blurred = banded(pad_along(along_y, 0), z_taps, 0, False)
        ratio = data / blurred
        back_z = banded(pad_along(ratio, 0), z_taps, 0, True)
        back_y = banded(pad_along(back_z, 2), y_taps, 2, True)
        back_x = banded(pad_along(back_y, 1), x_taps, 1, True)
        return total + back_x, None

    start = jnp.zeros(estimate.shape, jnp.float32)
    total, _ = lax.scan(one_view, start, (recorded, x_index, y_index, z_index, weights))
    return estimate * total / VIEWS
```

```python
import functools

import jax
import jax.numpy as jnp
from jax import lax
from jax.experimental import pallas as pl
from jax.experimental.pallas import tpu as pltpu
from jax.sharding import PartitionSpec as P

MESH = pl.DeviceIdType.MESH
ROWS = 8
GROUP = 8


def total_of(terms):
    total = None
    for term in terms:
        total = term if total is None else total + term
    return total


class Halo:
    def __init__(self, buffer, axis, size, count, width, plane_pieces, row_pieces, rows, sems):
        self.buffer, self.axis, self.count, self.width = buffer, axis, count, width
        self.plane_pieces, self.row_pieces, self.rows = plane_pieces, row_pieces, rows
        self.send, self.recv = sems
        here = lax.axis_index(axis)
        self.has = (here > 0, here < size - 1)
        self.to = (lax.max(here - 1, 0), lax.min(here + 1, size - 1))

    def copy(self, way, piece, row_piece):
        length = self.count // self.plane_pieces
        low, high = piece * length, (piece + 1) * length
        if way == 0:
            high = min(high, self.width)
            landing = self.count + self.width + low
        else:
            low = max(low, self.count - self.width)
            landing = low - (self.count - self.width)
        depth = self.rows // self.row_pieces
        rows = pl.ds(row_piece * depth, depth)
        slot = (way * self.plane_pieces + piece) * self.row_pieces + row_piece
        return pltpu.make_async_remote_copy(
            src_ref=self.buffer.at[pl.ds(self.width + low, high - low), rows],
            dst_ref=self.buffer.at[pl.ds(landing, high - low), rows],
            send_sem=self.send.at[slot],
            recv_sem=self.recv.at[slot],
            device_id={self.axis: self.to[way]},
            device_id_type=MESH,
        )

    def start(self, piece, row_piece):
        for way in (0, 1):
            @pl.when(self.has[way])
            def _():
                self.copy(way, piece, row_piece).start()

    def arrive(self, piece, row_piece):
        for way in (0, 1):
            @pl.when(self.has[1 - way])
            def _():
                self.copy(way, piece, row_piece).wait_recv()

    def finish(self):
        for way in (0, 1):
            @pl.when(self.has[way])
            def _():
                for piece in range(self.plane_pieces):
                    for row_piece in range(self.row_pieces):
                        self.copy(way, piece, row_piece).wait_send()

    def clear_ends(self):
        blank = jnp.zeros((self.width,) + self.buffer.shape[1:], self.buffer.dtype)

        @pl.when(jnp.logical_not(self.has[0]))
        def _():
            self.buffer[: self.width] = blank

        @pl.when(jnp.logical_not(self.has[1]))
        def _():
            self.buffer[self.count + self.width : self.count + 2 * self.width] = blank


def kernel(
    sizes, est, rec, xi, yi, zi, prof, out,
    ebuf, zbuf, rbuf, gbuf, tbuf, vbuf, table_in, table, wx, wy, wz,
    e_send, e_recv, z_send, z_recv, r_send, r_recv, g_send, g_recv, v_send, v_recv,
):
    views, tiles, slabs = sizes
    nz, nx, ny = est.shape
    directions, profs, taps = prof.shape[1:]
    half = taps // 2
    zparts, xparts = nz // ROWS, nx // ROWS
    e_halo = Halo(ebuf, "tile", tiles, nx, half, 1, zparts, nz, (e_send, e_recv))
    z_halo = Halo(zbuf, "slab", slabs, nz, half, zparts, xparts, nx, (z_send, z_recv))
    r_halo = Halo(rbuf, "slab", slabs, nz, half, 1, xparts, nx, (r_send, r_recv))
    g_halo = Halo(gbuf, "tile", tiles, nx, half, xparts, zparts, nz, (g_send, g_recv))
    view = lax.axis_index("view")

    barrier = pltpu.get_barrier_semaphore()
    heard = views - 1
    for halo in (e_halo, z_halo):
        for way in (0, 1):
            heard = heard + halo.has[way].astype(jnp.int32)

            @pl.when(halo.has[way])
            def _():
                pl.semaphore_signal(barrier, inc=1, device_id={halo.axis: halo.to[way]}, device_id_type=MESH)
    for step in range(1, views):
        pl.semaphore_signal(
            barrier, inc=1, device_id={"view": lax.rem(view + step, views)}, device_id_type=MESH
        )

    flat_est = est.reshape(nz * nx, ny)
    for x in range(nx):
        for zp in range(zparts):
            ebuf[half + x, pl.ds(zp * ROWS, ROWS), :] = flat_est[pl.ds(zp * ROWS * nx + x, ROWS, stride=nx), :]
    for halo in (e_halo, z_halo, r_halo, g_halo):
        halo.clear_ends()
    table_in[...] = jnp.zeros(table_in.shape, table_in.dtype)
    for a in range(directions):
        profile = prof[0, a]
        table_in[pl.ds(a * profs, profs), pl.ds(0, taps)] = profile / jnp.sum(profile, axis=-1, keepdims=True)
    table[...] = table_in[...].T

    pl.semaphore_wait(barrier, heard)
    for zp in range(zparts):
        e_halo.start(0, zp)

    def tap(k, index):
        row = jnp.broadcast_to(table[pl.ds(k, 1), :], (ROWS, table.shape[1]))
        return jnp.take_along_axis(row, index, axis=1, mode="promise_in_bounds")

    for zp in range(zparts):
        rows = pl.ds(zp * ROWS, ROWS)
        index = xi[0, rows, :]
        for k in range(taps):
            wx[k, rows, :] = tap(k, index)
    lane = lax.broadcasted_iota(jnp.int32, (ROWS, ny), 1)
    for zp in range(zparts):
        rows = pl.ds(zp * ROWS, ROWS)
        lines = yi[0, rows, :]
        for x in range(nx):
            index = jnp.broadcast_to(lines[:, x : x + 1], (ROWS, ny)) + profs
            for k in range(taps):
                read = lane + (k - half)
                wy[k, x, rows, :] = jnp.where((read >= 0) & (read < ny), tap(k, index), 0.0)
    for xp in range(xparts):
        rows = pl.ds(xp * ROWS, ROWS)
        index = zi[0, rows, :] + 2 * profs
        for k in range(taps):
            wz[k, rows, :] = tap(k, index)

    def blur(field, weights, first, rows, adjoint):
        taps_here = [weights[k, rows, :] for k in range(taps)]
        reads = [field[first + i, rows, :] for i in range(GROUP + taps - 1)]
        return [
            total_of(taps_here[k] * reads[i + (taps - 1 - k if adjoint else k)] for k in range(taps))
            for i in range(GROUP)
        ]

    flat_z = zbuf.reshape(zbuf.shape[0] * nx, ny)
    for zp in range(zparts):
        e_halo.arrive(0, zp)
        rows = pl.ds(zp * ROWS, ROWS)

        def forward(g, carry):
            first = g * GROUP
            for i, line in enumerate(blur(ebuf, wx, first, rows, False)):
                along_y = total_of(
                    wy[k, first + i, rows, :] * pltpu.roll(line, (half - k) % ny, 1) for k in range(taps)
                )
                flat_z[pl.ds((half + zp * ROWS) * nx + first + i, ROWS, stride=nx), :] = along_y
            return carry

        lax.fori_loop(0, nx // GROUP, forward, 0)
        for xp in range(xparts):
            z_halo.start(zp, xp)

    for xp in range(xparts):
        for zp in range(zparts):
            z_halo.arrive(zp, xp)
        rows = pl.ds(xp * ROWS, ROWS)

        def divide(g, carry):
            first = g * GROUP
            for i, blurred in enumerate(blur(zbuf, wz, first, rows, False)):
                rbuf[half + first + i, rows, :] = rec[0, first + i, rows, :] / blurred
            return carry

        lax.fori_loop(0, nz // GROUP, divide, 0)
        r_halo.start(0, xp)

    flat_t = tbuf.reshape(nz * nx, ny)
    for xp in range(xparts):
        r_halo.arrive(0, xp)
        rows = pl.ds(xp * ROWS, ROWS)

        def back_z(g, carry):
            first = g * GROUP
            for i, line in enumerate(blur(rbuf, wz, first, rows, True)):
                tbuf[first + i, rows, :] = line
            return carry

        lax.fori_loop(0, nz // GROUP, back_z, 0)
        for zp in range(zparts):
            z_rows = pl.ds(zp * ROWS, ROWS)

            def back_y(i, carry):
                x = xp * ROWS + i
                line = flat_t[pl.ds(zp * ROWS * nx + x, ROWS, stride=nx), :]
                gbuf[half + x, z_rows, :] = total_of(
                    pltpu.roll(wy[k, x, z_rows, :] * line, (k - half) % ny, 1) for k in range(taps)
                )
                return carry

            lax.fori_loop(0, ROWS, back_y, 0, unroll=4)
            g_halo.start(xp, zp)

    def view_copy(step, zp):
        piece = vbuf.at[view, pl.ds(zp * ROWS, ROWS)]
        slot = (step - 1) * zparts + zp
        return pltpu.make_async_remote_copy(
            src_ref=piece, dst_ref=piece, send_sem=v_send.at[slot], recv_sem=v_recv.at[slot],
            device_id={"view": lax.rem(view + step, views)}, device_id_type=MESH,
        )

    flat_v = vbuf.reshape(views * nz * nx, ny)
    for zp in range(zparts):
        for xp in range(xparts):
            g_halo.arrive(xp, zp)
        rows = pl.ds(zp * ROWS, ROWS)

        def back_x(g, carry):
            first = g * GROUP
            for i, line in enumerate(blur(gbuf, wx, first, rows, True)):
                flat_v[pl.ds((view * nz + zp * ROWS) * nx + first + i, ROWS, stride=nx), :] = line
            return carry

        lax.fori_loop(0, nx // GROUP, back_x, 0)
        for step in range(1, views):
            view_copy(step, zp).start()

    for zp in range(zparts):
        for step in range(1, views):
            view_copy(step, zp).wait_recv()
        planes = pl.ds(zp * ROWS, ROWS)
        out[planes] = est[planes] * total_of(vbuf[v, planes] for v in range(views)) / views

    for halo in (e_halo, z_halo, r_halo, g_halo):
        halo.finish()
    for zp in range(zparts):
        for step in range(1, views):
            view_copy(step, zp).wait_send()


def shards(sizes, estimate, recorded, x_index, y_index, z_index, profiles):
    views = sizes[0]
    nz, nx, ny = estimate.shape
    directions, profs, taps = profiles.shape[1:]
    assert recorded.shape[0] == 1
    half = taps // 2
    assert half <= min(nz, nx)
    assert directions * profs <= 128
    zparts, xparts = nz // ROWS, nx // ROWS
    f32 = jnp.float32
    counts = (zparts, zparts * xparts, xparts, zparts * xparts)
    sems = [pltpu.SemaphoreType.DMA((2 * c,)) for c in counts for _ in range(2)]
    sems += [pltpu.SemaphoreType.DMA((max(1, views - 1) * zparts,)) for _ in range(2)]
    return pl.pallas_call(
        functools.partial(kernel, sizes),
        out_shape=jax.ShapeDtypeStruct(estimate.shape, f32),
        in_specs=[pl.BlockSpec(memory_space=pltpu.VMEM)] * 6,
        out_specs=pl.BlockSpec(memory_space=pltpu.VMEM),
        scratch_shapes=[
            pltpu.VMEM((nx + 2 * half, nz, ny), f32),
            pltpu.VMEM((nz + 2 * half, nx, ny), f32),
            pltpu.VMEM((nz + 2 * half, nx, ny), f32),
            pltpu.VMEM((nx + 2 * half, nz, ny), f32),
            pltpu.VMEM((nz, nx, ny), f32),
            pltpu.VMEM((views, nz, nx, ny), f32),
            pltpu.VMEM((128, 128), f32),
            pltpu.VMEM((128, 128), f32),
            pltpu.VMEM((taps, nz, ny), f32),
            pltpu.VMEM((taps, nx, nz, ny), f32),
            pltpu.VMEM((taps, nx, ny), f32),
            *sems,
        ],
        compiler_params=pltpu.CompilerParams(
            collective_id=0, has_side_effects=True, vmem_limit_bytes=32 * 1024 * 1024
        ),
    )(estimate, recorded, x_index, y_index, z_index, profiles)


def solution(mesh):
    sizes = tuple(mesh.shape[name] for name in ("view", "tile", "slab"))
    placed = (
        P("slab", "tile", None),
        P("view", "slab", "tile", None),
        P("view", "slab", None),
        P("view", "slab", "tile"),
        P("view", "tile", None),
        P("view", None, None, None),
    )
    return jax.shard_map(
        functools.partial(shards, sizes),
        mesh=mesh, in_specs=placed, out_specs=P("slab", "tile", None), check_vma=False,
    )
```

```python
import functools

import jax
import jax.numpy as jnp
from jax import lax
from jax.experimental import pallas as pl
from jax.experimental.pallas import tpu as pltpu
from jax.sharding import PartitionSpec as P

MESH = pl.DeviceIdType.MESH
ROWS = 8
GROUP = 8


def total_of(terms):
    total = None
    for term in terms:
        total = term if total is None else total + term
    return total


class Halo:
    def __init__(self, buffer, axis, size, count, width, plane_pieces, row_pieces, rows, sems):
        self.buffer, self.axis, self.count, self.width = buffer, axis, count, width
        self.plane_pieces, self.row_pieces, self.rows = plane_pieces, row_pieces, rows
        self.send, self.recv = sems
        here = lax.axis_index(axis)
        self.has = (here > 0, here < size - 1)
        self.to = (lax.max(here - 1, 0), lax.min(here + 1, size - 1))

    def copy(self, way, piece, row_piece):
        length = self.count // self.plane_pieces
        low, high = piece * length, (piece + 1) * length
        if way == 0:
            high = min(high, self.width)
            landing = self.count + self.width + low
        else:
            low = max(low, self.count - self.width)
            landing = low - (self.count - self.width)
        depth = self.rows // self.row_pieces
        rows = pl.ds(row_piece * depth, depth)
        slot = (way * self.plane_pieces + piece) * self.row_pieces + row_piece
        return pltpu.make_async_remote_copy(
            src_ref=self.buffer.at[pl.ds(self.width + low, high - low), rows],
            dst_ref=self.buffer.at[pl.ds(landing, high - low), rows],
            send_sem=self.send.at[slot],
            recv_sem=self.recv.at[slot],
            device_id={self.axis: self.to[way]},
            device_id_type=MESH,
        )

    def start(self, piece, row_piece):
        for way in (0, 1):
            @pl.when(self.has[way])
            def _():
                self.copy(way, piece, row_piece).start()

    def arrive(self, piece, row_piece):
        for way in (0, 1):
            @pl.when(self.has[1 - way])
            def _():
                self.copy(way, piece, row_piece).wait_recv()

    def finish(self):
        for way in (0, 1):
            @pl.when(self.has[way])
            def _():
                for piece in range(self.plane_pieces):
                    for row_piece in range(self.row_pieces):
                        self.copy(way, piece, row_piece).wait_send()

    def clear_ends(self):
        blank = jnp.zeros((self.width,) + self.buffer.shape[1:], self.buffer.dtype)

        @pl.when(jnp.logical_not(self.has[0]))
        def _():
            self.buffer[: self.width] = blank

        @pl.when(jnp.logical_not(self.has[1]))
        def _():
            self.buffer[self.count + self.width : self.count + 2 * self.width] = blank


def kernel(
    sizes, est_hbm, rec_hbm, xi_hbm, yi_hbm, zi_hbm, prof_hbm, out,
    est, rec, xi, yi, zi, prof, in_sems, ebuf, zbuf, rbuf, gbuf, tbuf, vbuf, table_in, table, wx, wy, wz,
    e_send, e_recv, z_send, z_recv, r_send, r_recv, g_send, g_recv, v_send, v_recv,
):
    views, tiles, slabs = sizes
    sources = (est_hbm, prof_hbm, xi_hbm, yi_hbm, zi_hbm, rec_hbm)
    fetches = [
        pltpu.make_async_copy(source, target, in_sems.at[i])
        for i, (source, target) in enumerate(zip(sources, (est, prof, xi, yi, zi, rec)))
    ]
    for fetch in fetches:
        fetch.start()
    fetch_est, *fetch_taps, fetch_rec = fetches
    nz, nx, ny = est.shape
    directions, profs, taps = prof.shape[1:]
    half = taps // 2
    zparts, xparts = nz // ROWS, nx // ROWS
    e_halo = Halo(ebuf, "tile", tiles, nx, half, 1, zparts, nz, (e_send, e_recv))
    z_halo = Halo(zbuf, "slab", slabs, nz, half, zparts, xparts, nx, (z_send, z_recv))
    r_halo = Halo(rbuf, "slab", slabs, nz, half, 1, xparts, nx, (r_send, r_recv))
    g_halo = Halo(gbuf, "tile", tiles, nx, half, xparts, zparts, nz, (g_send, g_recv))
    view = lax.axis_index("view")

    barrier = pltpu.get_barrier_semaphore()
    heard = views - 1
    for halo in (e_halo, z_halo):
        for way in (0, 1):
            heard = heard + halo.has[way].astype(jnp.int32)

            @pl.when(halo.has[way])
            def _():
                pl.semaphore_signal(barrier, inc=1, device_id={halo.axis: halo.to[way]}, device_id_type=MESH)
    for step in range(1, views):
        pl.semaphore_signal(
            barrier, inc=1, device_id={"view": lax.rem(view + step, views)}, device_id_type=MESH
        )

    fetch_est.wait()
    flat_est = est.reshape(nz * nx, ny)
    for x in range(nx):
        for zp in range(zparts):
            ebuf[half + x, pl.ds(zp * ROWS, ROWS), :] = flat_est[pl.ds(zp * ROWS * nx + x, ROWS, stride=nx), :]
    for halo in (e_halo, z_halo, r_halo, g_halo):
        halo.clear_ends()
    for fetch in fetch_taps:
        fetch.wait()
    table_in[...] = jnp.zeros(table_in.shape, table_in.dtype)
    for a in range(directions):
        profile = prof[0, a]
        table_in[pl.ds(a * profs, profs), pl.ds(0, taps)] = profile / jnp.sum(profile, axis=-1, keepdims=True)
    table[...] = table_in[...].T

    pl.semaphore_wait(barrier, heard)
    for zp in range(zparts):
        e_halo.start(0, zp)

    def tap(k, index):
        row = jnp.broadcast_to(table[pl.ds(k, 1), :], (ROWS, table.shape[1]))
        return jnp.take_along_axis(row, index, axis=1, mode="promise_in_bounds")

    for zp in range(zparts):
        rows = pl.ds(zp * ROWS, ROWS)
        index = xi[0, rows, :]
        for k in range(taps):
            wx[k, rows, :] = tap(k, index)
    lane = lax.broadcasted_iota(jnp.int32, (ROWS, ny), 1)
    for zp in range(zparts):
        rows = pl.ds(zp * ROWS, ROWS)
        lines = yi[0, rows, :]
        for x in range(nx):
            index = jnp.broadcast_to(lines[:, x : x + 1], (ROWS, ny)) + profs
            for k in range(taps):
                read = lane + (k - half)
                wy[k, x, rows, :] = jnp.where((read >= 0) & (read < ny), tap(k, index), 0.0)
    for xp in range(xparts):
        rows = pl.ds(xp * ROWS, ROWS)
        index = zi[0, rows, :] + 2 * profs
        for k in range(taps):
            wz[k, rows, :] = tap(k, index)

    def blur(field, weights, first, rows, adjoint):
        taps_here = [weights[k, rows, :] for k in range(taps)]
        reads = [field[first + i, rows, :] for i in range(GROUP + taps - 1)]
        return [
            total_of(taps_here[k] * reads[i + (taps - 1 - k if adjoint else k)] for k in range(taps))
            for i in range(GROUP)
        ]

    fetch_rec.wait()
    flat_z = zbuf.reshape(zbuf.shape[0] * nx, ny)
    for zp in range(zparts):
        e_halo.arrive(0, zp)
        rows = pl.ds(zp * ROWS, ROWS)

        def forward(g, carry):
            first = g * GROUP
            for i, line in enumerate(blur(ebuf, wx, first, rows, False)):
                along_y = total_of(
                    wy[k, first + i, rows, :] * pltpu.roll(line, (half - k) % ny, 1) for k in range(taps)
                )
                flat_z[pl.ds((half + zp * ROWS) * nx + first + i, ROWS, stride=nx), :] = along_y
            return carry

        lax.fori_loop(0, nx // GROUP, forward, 0)
        for xp in range(xparts):
            z_halo.start(zp, xp)

    for xp in range(xparts):
        for zp in range(zparts):
            z_halo.arrive(zp, xp)
        rows = pl.ds(xp * ROWS, ROWS)

        def divide(g, carry):
            first = g * GROUP
            for i, blurred in enumerate(blur(zbuf, wz, first, rows, False)):
                rbuf[half + first + i, rows, :] = rec[0, first + i, rows, :] / blurred
            return carry

        lax.fori_loop(0, nz // GROUP, divide, 0)
        r_halo.start(0, xp)

    flat_t = tbuf.reshape(nz * nx, ny)
    for xp in range(xparts):
        r_halo.arrive(0, xp)
        rows = pl.ds(xp * ROWS, ROWS)

        def back_z(g, carry):
            first = g * GROUP
            for i, line in enumerate(blur(rbuf, wz, first, rows, True)):
                tbuf[first + i, rows, :] = line
            return carry

        lax.fori_loop(0, nz // GROUP, back_z, 0)
        for zp in range(zparts):
            z_rows = pl.ds(zp * ROWS, ROWS)

            def back_y(i, carry):
                x = xp * ROWS + i
                line = flat_t[pl.ds(zp * ROWS * nx + x, ROWS, stride=nx), :]
                gbuf[half + x, z_rows, :] = total_of(
                    pltpu.roll(wy[k, x, z_rows, :] * line, (k - half) % ny, 1) for k in range(taps)
                )
                return carry

            lax.fori_loop(0, ROWS, back_y, 0, unroll=4)
            g_halo.start(xp, zp)

    def view_copy(step, zp):
        piece = vbuf.at[view, pl.ds(zp * ROWS, ROWS)]
        slot = (step - 1) * zparts + zp
        return pltpu.make_async_remote_copy(
            src_ref=piece, dst_ref=piece, send_sem=v_send.at[slot], recv_sem=v_recv.at[slot],
            device_id={"view": lax.rem(view + step, views)}, device_id_type=MESH,
        )

    flat_v = vbuf.reshape(views * nz * nx, ny)
    for zp in range(zparts):
        for xp in range(xparts):
            g_halo.arrive(xp, zp)
        rows = pl.ds(zp * ROWS, ROWS)

        def back_x(g, carry):
            first = g * GROUP
            for i, line in enumerate(blur(gbuf, wx, first, rows, True)):
                flat_v[pl.ds((view * nz + zp * ROWS) * nx + first + i, ROWS, stride=nx), :] = line
            return carry

        lax.fori_loop(0, nx // GROUP, back_x, 0)
        for step in range(1, views):
            view_copy(step, zp).start()

    for zp in range(zparts):
        for step in range(1, views):
            view_copy(step, zp).wait_recv()
        planes = pl.ds(zp * ROWS, ROWS)
        out[planes] = est[planes] * total_of(vbuf[v, planes] for v in range(views)) / views

    for halo in (e_halo, z_halo, r_halo, g_halo):
        halo.finish()
    for zp in range(zparts):
        for step in range(1, views):
            view_copy(step, zp).wait_send()


def shards(sizes, *args):
    estimate, recorded, x_index, y_index, z_index, profiles = args
    views = sizes[0]
    nz, nx, ny = estimate.shape
    directions, profs, taps = profiles.shape[1:]
    assert recorded.shape[0] == 1
    half = taps // 2
    assert half <= min(nz, nx)
    assert directions * profs <= 128
    zparts, xparts = nz // ROWS, nx // ROWS
    f32 = jnp.float32
    counts = (zparts, zparts * xparts, xparts, zparts * xparts)
    sems = [pltpu.SemaphoreType.DMA((2 * c,)) for c in counts for _ in range(2)]
    sems += [pltpu.SemaphoreType.DMA((max(1, views - 1) * zparts,)) for _ in range(2)]
    return pl.pallas_call(
        functools.partial(kernel, sizes),
        out_shape=jax.ShapeDtypeStruct(estimate.shape, f32),
        in_specs=[pl.BlockSpec(memory_space=pltpu.HBM)] * 6,
        out_specs=pl.BlockSpec(memory_space=pltpu.VMEM),
        scratch_shapes=[
            *(pltpu.VMEM(a.shape, a.dtype) for a in args),
            pltpu.SemaphoreType.DMA((len(args),)),
            pltpu.VMEM((nx + 2 * half, nz, ny), f32),
            pltpu.VMEM((nz + 2 * half, nx, ny), f32),
            pltpu.VMEM((nz + 2 * half, nx, ny), f32),
            pltpu.VMEM((nx + 2 * half, nz, ny), f32),
            pltpu.VMEM((nz, nx, ny), f32),
            pltpu.VMEM((views, nz, nx, ny), f32),
            pltpu.VMEM((128, 128), f32),
            pltpu.VMEM((128, 128), f32),
            pltpu.VMEM((taps, nz, ny), f32),
            pltpu.VMEM((taps, nx, nz, ny), f32),
            pltpu.VMEM((taps, nx, ny), f32),
            *sems,
        ],
        compiler_params=pltpu.CompilerParams(
            collective_id=0, has_side_effects=True, vmem_limit_bytes=67_043_328
        ),
    )(*args)


def solution(mesh):
    sizes = tuple(mesh.shape[name] for name in ("view", "tile", "slab"))
    placed = (
        P("slab", "tile", None),
        P("view", "slab", "tile", None),
        P("view", "slab", None),
        P("view", "slab", "tile"),
        P("view", "tile", None),
        P("view", None, None, None),
    )
    return jax.shard_map(
        functools.partial(shards, sizes),
        mesh=mesh, in_specs=placed, out_specs=P("slab", "tile", None), check_vma=False,
    )
```

```python
import functools

import jax
import jax.numpy as jnp
from jax import lax
from jax.experimental import pallas as pl
from jax.experimental.pallas import tpu as pltpu
from jax.sharding import PartitionSpec as P

MESH = pl.DeviceIdType.MESH
ROWS = 8
GROUP = 8


def total_of(terms):
    total = None
    for term in terms:
        total = term if total is None else total + term
    return total


def estimate_copy(halo, source, landing, sems, way, piece):
    planes = pl.ds(piece * ROWS, ROWS)
    slot = way * (source.shape[0] // ROWS) + piece
    return pltpu.make_async_remote_copy(
        src_ref=source.at[planes], dst_ref=landing.at[way, planes],
        send_sem=sems[0].at[slot], recv_sem=sems[1].at[slot],
        device_id={halo.axis: halo.to[way]}, device_id_type=MESH,
    )


class Halo:
    def __init__(self, buffer, axis, size, count, width, plane_pieces, row_pieces, rows, sems):
        self.buffer, self.axis, self.count, self.width = buffer, axis, count, width
        self.plane_pieces, self.row_pieces, self.rows = plane_pieces, row_pieces, rows
        self.send, self.recv = sems
        here = lax.axis_index(axis)
        self.has = (here > 0, here < size - 1)
        self.to = (lax.max(here - 1, 0), lax.min(here + 1, size - 1))

    def copy(self, way, piece, row_piece):
        length = self.count // self.plane_pieces
        low, high = piece * length, (piece + 1) * length
        if way == 0:
            high = min(high, self.width)
            landing = self.count + self.width + low
        else:
            low = max(low, self.count - self.width)
            landing = low - (self.count - self.width)
        depth = self.rows // self.row_pieces
        rows = pl.ds(row_piece * depth, depth)
        slot = (way * self.plane_pieces + piece) * self.row_pieces + row_piece
        return pltpu.make_async_remote_copy(
            src_ref=self.buffer.at[pl.ds(self.width + low, high - low), rows],
            dst_ref=self.buffer.at[pl.ds(landing, high - low), rows],
            send_sem=self.send.at[slot],
            recv_sem=self.recv.at[slot],
            device_id={self.axis: self.to[way]},
            device_id_type=MESH,
        )

    def start(self, piece, row_piece):
        for way in (0, 1):
            @pl.when(self.has[way])
            def _():
                self.copy(way, piece, row_piece).start()

    def arrive(self, piece, row_piece):
        for way in (0, 1):
            @pl.when(self.has[1 - way])
            def _():
                self.copy(way, piece, row_piece).wait_recv()

    def finish(self):
        for way in (0, 1):
            @pl.when(self.has[way])
            def _():
                for piece in range(self.plane_pieces):
                    for row_piece in range(self.row_pieces):
                        self.copy(way, piece, row_piece).wait_send()

    def clear_ends(self):
        blank = jnp.zeros((self.width,) + self.buffer.shape[1:], self.buffer.dtype)

        @pl.when(jnp.logical_not(self.has[0]))
        def _():
            self.buffer[: self.width] = blank

        @pl.when(jnp.logical_not(self.has[1]))
        def _():
            self.buffer[self.count + self.width : self.count + 2 * self.width] = blank


def kernel(
    sizes, est_hbm, rec_hbm, xi_hbm, yi_hbm, zi_hbm, prof_hbm, out,
    est, rec, xi, yi, zi, prof, in_sems, eland, ebuf, zbuf, rbuf, gbuf, tbuf, vbuf, table_in, table, wx, wy, wz,
    e_send, e_recv, z_send, z_recv, r_send, r_recv, g_send, g_recv, v_send, v_recv,
):
    views, tiles, slabs = sizes
    sources = (est_hbm, prof_hbm, xi_hbm, yi_hbm, zi_hbm, rec_hbm)
    fetches = [
        pltpu.make_async_copy(source, target, in_sems.at[i])
        for i, (source, target) in enumerate(zip(sources, (est, prof, xi, yi, zi, rec)))
    ]
    for fetch in fetches:
        fetch.start()
    fetch_est, *fetch_taps, fetch_rec = fetches
    nz, nx, ny = est.shape
    directions, profs, taps = prof.shape[1:]
    half = taps // 2
    zparts, xparts = nz // ROWS, nx // ROWS
    z_halo = Halo(zbuf, "slab", slabs, nz, half, zparts, xparts, nx, (z_send, z_recv))
    r_halo = Halo(rbuf, "slab", slabs, nz, half, 1, xparts, nx, (r_send, r_recv))
    g_halo = Halo(gbuf, "tile", tiles, nx, half, xparts, zparts, nz, (g_send, g_recv))
    view = lax.axis_index("view")

    barrier = pltpu.get_barrier_semaphore()
    heard = views - 1
    for halo in (g_halo, z_halo):
        for way in (0, 1):
            heard = heard + halo.has[way].astype(jnp.int32)

            @pl.when(halo.has[way])
            def _():
                pl.semaphore_signal(barrier, inc=1, device_id={halo.axis: halo.to[way]}, device_id_type=MESH)
    for step in range(1, views):
        pl.semaphore_signal(
            barrier, inc=1, device_id={"view": lax.rem(view + step, views)}, device_id_type=MESH
        )

    pl.semaphore_wait(barrier, heard)
    e_copy = functools.partial(estimate_copy, g_halo, est_hbm, eland, (e_send, e_recv))
    for zp in range(zparts):
        for way in (0, 1):
            @pl.when(g_halo.has[way])
            def _():
                e_copy(way, zp).start()

    for halo in (z_halo, r_halo, g_halo):
        halo.clear_ends()
    for fetch in fetch_taps:
        fetch.wait()
    table_in[...] = jnp.zeros(table_in.shape, table_in.dtype)
    for a in range(directions):
        profile = prof[0, a]
        table_in[pl.ds(a * profs, profs), pl.ds(0, taps)] = profile / jnp.sum(profile, axis=-1, keepdims=True)
    table[...] = table_in[...].T

    steps = int(taps**0.5) + 1

    def coarse_of(k):
        return (k - half) // steps * steps

    def y_forward(line, x, rows):
        shifted, partial = {}, {}
        for k in range(taps):
            coarse = coarse_of(k)
            fine = k - half - coarse
            if fine not in shifted:
                shifted[fine] = pltpu.roll(line, -fine % ny, 1) if fine else line
            term = wy[k, x, rows, :] * shifted[fine]
            partial[coarse] = partial[coarse] + term if coarse in partial else term
        return total_of(pltpu.roll(v, -c % ny, 1) if c else v for c, v in partial.items())

    def y_back(line, x, rows):
        shifted, partial = {}, {}
        for k in range(taps):
            coarse = coarse_of(k)
            fine = k - half - coarse
            if coarse not in shifted:
                shifted[coarse] = pltpu.roll(line, coarse % ny, 1) if coarse else line
            term = wy[k, x, rows, :] * shifted[coarse]
            partial[fine] = partial[fine] + term if fine in partial else term
        return total_of(pltpu.roll(v, f, 1) if f else v for f, v in partial.items())

    def tap(k, index):
        row = jnp.broadcast_to(table[pl.ds(k, 1), :], (ROWS, table.shape[1]))
        return jnp.take_along_axis(row, index, axis=1, mode="promise_in_bounds")

    for zp in range(zparts):
        rows = pl.ds(zp * ROWS, ROWS)
        index = xi[0, rows, :]
        for k in range(taps):
            wx[k, rows, :] = tap(k, index)
    lane = lax.broadcasted_iota(jnp.int32, (ROWS, ny), 1)
    inside = []
    for k in range(taps):
        read = lax.rem(lane + (ny - coarse_of(k)), ny) + (k - half)
        inside.append((read >= 0) & (read < ny))
    for zp in range(zparts):
        rows = pl.ds(zp * ROWS, ROWS)
        lines = yi[0, rows, :]
        for x in range(nx):
            index = jnp.broadcast_to(lines[:, x : x + 1], (ROWS, ny)) + profs
            for k in range(taps):
                wy[k, x, rows, :] = jnp.where(inside[k], tap(k, index), 0.0)
    for xp in range(xparts):
        rows = pl.ds(xp * ROWS, ROWS)
        index = zi[0, rows, :] + 2 * profs
        for k in range(taps):
            wz[k, rows, :] = tap(k, index)

    def blur(field, weights, first, rows, adjoint):
        taps_here = [weights[k, rows, :] for k in range(taps)]
        reads = [field[first + i, rows, :] for i in range(GROUP + taps - 1)]
        return [
            total_of(taps_here[k] * reads[i + (taps - 1 - k if adjoint else k)] for k in range(taps))
            for i in range(GROUP)
        ]

    def turn(source, planes, zp, first, at):
        for i in range(planes):
            line = source[pl.ds(zp * ROWS * nx + first + i, ROWS, stride=nx), :]
            ebuf[at + i, pl.ds(zp * ROWS, ROWS), :] = line

    fetch_est.wait()
    for zp in range(zparts):
        turn(est.reshape(nz * nx, ny), nx, zp, 0, half)
    fetch_rec.wait()
    flat_z = zbuf.reshape(zbuf.shape[0] * nx, ny)
    for zp in range(zparts):
        rows = pl.ds(zp * ROWS, ROWS)
        for way, first, at in ((0, 0, half + nx), (1, nx - half, 0)):
            @pl.when(g_halo.has[1 - way])
            def _():
                e_copy(way, zp).wait_recv()
                turn(eland.at[way].reshape(nz * nx, ny), half, zp, first, at)

            @pl.when(jnp.logical_not(g_halo.has[1 - way]))
            def _():
                ebuf[at : at + half, rows, :] = jnp.zeros((half, ROWS, ny), ebuf.dtype)

        def forward(g, carry):
            first = g * GROUP
            for i, line in enumerate(blur(ebuf, wx, first, rows, False)):
                spot = (half + zp * ROWS) * nx + first + i
                flat_z[pl.ds(spot, ROWS, stride=nx), :] = y_forward(line, first + i, rows)
            return carry

        lax.fori_loop(0, nx // GROUP, forward, 0)
        for xp in range(xparts):
            z_halo.start(zp, xp)

    for xp in range(xparts):
        for zp in range(zparts):
            z_halo.arrive(zp, xp)
        rows = pl.ds(xp * ROWS, ROWS)

        def divide(g, carry):
            first = g * GROUP
            for i, blurred in enumerate(blur(zbuf, wz, first, rows, False)):
                rbuf[half + first + i, rows, :] = rec[0, first + i, rows, :] / blurred
            return carry

        lax.fori_loop(0, nz // GROUP, divide, 0)
        r_halo.start(0, xp)

    flat_t = tbuf.reshape(nz * nx, ny)
    for zp in range(zparts):
        z_rows = pl.ds(zp * ROWS, ROWS)
        for xp in range(xparts):
            rows = pl.ds(xp * ROWS, ROWS)

            def back_z(g, carry):
                first = g * GROUP
                for i, line in enumerate(blur(rbuf, wz, first, rows, True)):
                    tbuf[first + i, rows, :] = line
                return carry

            if zp == 0:
                r_halo.arrive(0, xp)
                lax.fori_loop(0, nz // GROUP, back_z, 0)

            def back_y(i, carry):
                x = xp * ROWS + i
                line = flat_t[pl.ds(zp * ROWS * nx + x, ROWS, stride=nx), :]
                gbuf[half + x, z_rows, :] = y_back(line, x, z_rows)
                return carry

            lax.fori_loop(0, ROWS, back_y, 0, unroll=4)
            g_halo.start(xp, zp)

    def view_copy(step, zp):
        piece = vbuf.at[view, pl.ds(zp * ROWS, ROWS)]
        slot = (step - 1) * zparts + zp
        return pltpu.make_async_remote_copy(
            src_ref=piece, dst_ref=piece, send_sem=v_send.at[slot], recv_sem=v_recv.at[slot],
            device_id={"view": lax.rem(view + step, views)}, device_id_type=MESH,
        )

    flat_v = vbuf.reshape(views * nz * nx, ny)
    for zp in range(zparts):
        for xp in range(xparts):
            g_halo.arrive(xp, zp)
        rows = pl.ds(zp * ROWS, ROWS)

        def back_x(g, carry):
            first = g * GROUP
            for i, line in enumerate(blur(gbuf, wx, first, rows, True)):
                flat_v[pl.ds((view * nz + zp * ROWS) * nx + first + i, ROWS, stride=nx), :] = line
            return carry

        lax.fori_loop(0, nx // GROUP, back_x, 0)
        for step in range(1, views):
            view_copy(step, zp).start()

    for zp in range(zparts):
        for step in range(1, views):
            view_copy(step, zp).wait_recv()
        planes = pl.ds(zp * ROWS, ROWS)
        out[planes] = est[planes] * total_of(vbuf[v, planes] for v in range(views)) / views

    for halo in (z_halo, r_halo, g_halo):
        halo.finish()
    for way in (0, 1):
        @pl.when(g_halo.has[way])
        def _():
            for zp in range(zparts):
                e_copy(way, zp).wait_send()
    for zp in range(zparts):
        for step in range(1, views):
            view_copy(step, zp).wait_send()


def shards(sizes, *args):
    estimate, recorded, x_index, y_index, z_index, profiles = args
    views = sizes[0]
    nz, nx, ny = estimate.shape
    directions, profs, taps = profiles.shape[1:]
    assert recorded.shape[0] == 1
    half = taps // 2
    assert half <= min(nz, nx)
    assert directions * profs <= 128
    zparts, xparts = nz // ROWS, nx // ROWS
    f32 = jnp.float32
    counts = (zparts, zparts * xparts, xparts, zparts * xparts)
    sems = [pltpu.SemaphoreType.DMA((2 * c,)) for c in counts for _ in range(2)]
    sems += [pltpu.SemaphoreType.DMA((max(1, views - 1) * zparts,)) for _ in range(2)]
    return pl.pallas_call(
        functools.partial(kernel, sizes),
        out_shape=jax.ShapeDtypeStruct(estimate.shape, f32),
        in_specs=[pl.BlockSpec(memory_space=pltpu.HBM)] * 6,
        out_specs=pl.BlockSpec(memory_space=pltpu.VMEM),
        scratch_shapes=[
            *(pltpu.VMEM(a.shape, a.dtype) for a in args),
            pltpu.SemaphoreType.DMA((len(args),)),
            pltpu.VMEM((2, nz, nx, ny), f32),
            pltpu.VMEM((nx + 2 * half, nz, ny), f32),
            pltpu.VMEM((nz + 2 * half, nx, ny), f32),
            pltpu.VMEM((nz + 2 * half, nx, ny), f32),
            pltpu.VMEM((nx + 2 * half, nz, ny), f32),
            pltpu.VMEM((nz, nx, ny), f32),
            pltpu.VMEM((views, nz, nx, ny), f32),
            pltpu.VMEM((128, 128), f32),
            pltpu.VMEM((128, 128), f32),
            pltpu.VMEM((taps, nz, ny), f32),
            pltpu.VMEM((taps, nx, nz, ny), f32),
            pltpu.VMEM((taps, nx, ny), f32),
            *sems,
        ],
        compiler_params=pltpu.CompilerParams(
            collective_id=0, has_side_effects=True, vmem_limit_bytes=32 * 1024 * 1024
        ),
    )(*(pltpu.with_memory_space_constraint(a, pltpu.HBM) for a in args))


def solution(mesh):
    sizes = tuple(mesh.shape[name] for name in ("view", "tile", "slab"))
    placed = (
        P("slab", "tile", None),
        P("view", "slab", "tile", None),
        P("view", "slab", None),
        P("view", "slab", "tile"),
        P("view", "tile", None),
        P("view", None, None, None),
    )
    return jax.shard_map(
        functools.partial(shards, sizes),
        mesh=mesh, in_specs=placed, out_specs=P("slab", "tile", None), check_vma=False,
    )
```

```python
import functools

import jax
import jax.numpy as jnp
from jax import lax
from jax.experimental import pallas as pl
from jax.experimental.pallas import tpu as pltpu
from jax.sharding import PartitionSpec as P

MESH = pl.DeviceIdType.MESH
ROWS = 8
GROUP = ROWS


def total_of(terms):
    total = None
    for term in terms:
        total = term if total is None else total + term
    return total


def estimate_copy(halo, source, landing, sems, way, piece):
    planes = pl.ds(piece * ROWS, ROWS)
    slot = way * (source.shape[0] // ROWS) + piece
    return pltpu.make_async_remote_copy(
        src_ref=source.at[planes], dst_ref=landing.at[way, planes],
        send_sem=sems[0].at[slot], recv_sem=sems[1].at[slot],
        device_id={halo.axis: halo.to[way]}, device_id_type=MESH,
    )


class Halo:
    def __init__(self, buffer, axis, size, count, width, plane_pieces, row_pieces, rows, sems):
        self.buffer, self.axis, self.count, self.width = buffer, axis, count, width
        self.plane_pieces, self.row_pieces, self.rows = plane_pieces, row_pieces, rows
        self.send, self.recv = sems
        self.waited = set()
        here = lax.axis_index(axis)
        self.has = (here > 0, here < size - 1)
        self.to = (lax.max(here - 1, 0), lax.min(here + 1, size - 1))

    def planes(self, way, piece):
        length = self.count // self.plane_pieces
        low, high = piece * length, (piece + 1) * length
        if way == 0:
            high = min(high, self.width)
            return low, high, self.count + self.width + low
        low = max(low, self.count - self.width)
        return low, high, low - (self.count - self.width)

    def copy(self, way, piece, row_piece):
        low, high, landing = self.planes(way, piece)
        depth = self.rows // self.row_pieces
        rows = pl.ds(row_piece * depth, depth)
        slot = (way * self.plane_pieces + piece) * self.row_pieces + row_piece
        return pltpu.make_async_remote_copy(
            src_ref=self.buffer.at[pl.ds(self.width + low, high - low), rows],
            dst_ref=self.buffer.at[pl.ds(landing, high - low), rows],
            send_sem=self.send.at[slot],
            recv_sem=self.recv.at[slot],
            device_id={self.axis: self.to[way]},
            device_id_type=MESH,
        )

    def start(self, piece, row_piece):
        for way in (0, 1):
            @pl.when(self.has[way])
            def _():
                self.copy(way, piece, row_piece).start()

    def need(self, first, last, row_piece):
        for way in (0, 1):
            fresh = []
            for piece in range(self.plane_pieces):
                low, high, landing = self.planes(way, piece)
                spot = (way, piece, row_piece)
                if landing < last and landing + high - low > first and spot not in self.waited:
                    self.waited.add(spot)
                    fresh.append(piece)
            if fresh:
                @pl.when(self.has[1 - way])
                def _():
                    for piece in fresh:
                        self.copy(way, piece, row_piece).wait_recv()

    def finish(self):
        for way in (0, 1):
            @pl.when(self.has[way])
            def _():
                for piece in range(self.plane_pieces):
                    for row_piece in range(self.row_pieces):
                        self.copy(way, piece, row_piece).wait_send()

    def clear_ends(self):
        blank = jnp.zeros((self.width,) + self.buffer.shape[1:], self.buffer.dtype)

        @pl.when(jnp.logical_not(self.has[0]))
        def _():
            self.buffer[: self.width] = blank

        @pl.when(jnp.logical_not(self.has[1]))
        def _():
            self.buffer[self.count + self.width : self.count + 2 * self.width] = blank


def kernel(
    sizes, est_hbm, rec_hbm, xi_hbm, yi_hbm, zi_hbm, prof_hbm, out,
    est, rec, xi, yi, zi, prof, in_sems, eland, ebuf, zbuf, rbuf, gbuf, tbuf, vbuf, table_in, table, wx, wy, wz,
    e_send, e_recv, z_send, z_recv, r_send, r_recv, g_send, g_recv, v_send, v_recv,
):
    views, tiles, slabs = sizes
    sources = (est_hbm, prof_hbm, xi_hbm, yi_hbm, zi_hbm, rec_hbm)
    fetches = [
        pltpu.make_async_copy(source, target, in_sems.at[i])
        for i, (source, target) in enumerate(zip(sources, (est, prof, xi, yi, zi, rec)))
    ]
    fetch_est, *fetch_taps, fetch_rec = fetches
    nz, nx, ny = est.shape
    directions, profs, taps = prof.shape[1:]
    half = taps // 2
    zparts, xparts = nz // ROWS, nx // ROWS
    z_halo = Halo(zbuf, "slab", slabs, nz, half, zparts, xparts, nx, (z_send, z_recv))
    r_halo = Halo(rbuf, "slab", slabs, nz, half, zparts, xparts, nx, (r_send, r_recv))
    g_halo = Halo(gbuf, "tile", tiles, nx, half, xparts, zparts, nz, (g_send, g_recv))
    view = lax.axis_index("view")

    barrier = pltpu.get_barrier_semaphore()
    heard = views - 1
    for halo in (g_halo, z_halo):
        for way in (0, 1):
            heard = heard + halo.has[way].astype(jnp.int32)

            @pl.when(halo.has[way])
            def _():
                pl.semaphore_signal(barrier, inc=1, device_id={halo.axis: halo.to[way]}, device_id_type=MESH)
    for step in range(1, views):
        pl.semaphore_signal(
            barrier, inc=1, device_id={"view": lax.rem(view + step, views)}, device_id_type=MESH
        )

    for fetch in fetch_taps:
        fetch.start()
    pl.semaphore_wait(barrier, heard)
    e_copy = functools.partial(estimate_copy, g_halo, est_hbm, eland, (e_send, e_recv))
    for zp in range(zparts):
        for way in (0, 1):
            @pl.when(g_halo.has[way])
            def _():
                e_copy(way, zp).start()

    fetch_est.start()
    fetch_rec.start()

    for halo in (z_halo, r_halo, g_halo):
        halo.clear_ends()
    for fetch in fetch_taps:
        fetch.wait()
    table_in[...] = jnp.zeros(table_in.shape, table_in.dtype)
    for a in range(directions):
        profile = prof[0, a]
        table_in[pl.ds(a * profs, profs), pl.ds(0, taps)] = profile / jnp.sum(profile, axis=-1, keepdims=True)
    table[...] = table_in[...].T

    steps = int(taps**0.5) + 1

    def coarse_of(k):
        return (k - half) // steps * steps

    def y_forward(line, x, rows):
        shifted, partial = {}, {}
        for k in range(taps):
            coarse = coarse_of(k)
            fine = k - half - coarse
            if fine not in shifted:
                shifted[fine] = pltpu.roll(line, -fine % ny, 1) if fine else line
            term = wy[k, x, rows, :] * shifted[fine]
            partial[coarse] = partial[coarse] + term if coarse in partial else term
        return total_of(pltpu.roll(v, -c % ny, 1) if c else v for c, v in partial.items())

    def y_back(line, x, rows):
        shifted, partial = {}, {}
        for k in range(taps):
            coarse = coarse_of(k)
            fine = k - half - coarse
            if coarse not in shifted:
                shifted[coarse] = pltpu.roll(line, coarse % ny, 1) if coarse else line
            term = wy[k, x, rows, :] * shifted[coarse]
            partial[fine] = partial[fine] + term if fine in partial else term
        return total_of(pltpu.roll(v, f, 1) if f else v for f, v in partial.items())

    def tap(k, index):
        row = jnp.broadcast_to(table[pl.ds(k, 1), :], (ROWS, table.shape[1]))
        return jnp.take_along_axis(row, index, axis=1, mode="promise_in_bounds")

    for zp in range(zparts):
        rows = pl.ds(zp * ROWS, ROWS)
        index = xi[0, rows, :]
        for k in range(taps):
            wx[k, rows, :] = tap(k, index)
    lane = lax.broadcasted_iota(jnp.int32, (ROWS, ny), 1)
    inside = []
    for k in range(taps):
        read = lax.rem(lane + (ny - coarse_of(k)), ny) + (k - half)
        inside.append((read >= 0) & (read < ny))
    for zp in range(zparts):
        rows = pl.ds(zp * ROWS, ROWS)
        lines = yi[0, rows, :]
        for x in range(nx):
            index = jnp.broadcast_to(lines[:, x : x + 1], (ROWS, ny)) + profs
            for k in range(taps):
                wy[k, x, rows, :] = jnp.where(inside[k], tap(k, index), 0.0)
    def blur(field, weights, first, rows, adjoint):
        taps_here = [weights[k, rows, :] for k in range(taps)]
        reads = [field[first + i, rows, :] for i in range(GROUP + taps - 1)]
        return [
            total_of(taps_here[k] * reads[i + (taps - 1 - k if adjoint else k)] for k in range(taps))
            for i in range(GROUP)
        ]

    def turn(source, planes, zp, first, at):
        for i in range(planes):
            line = source[pl.ds(zp * ROWS * nx + first + i, ROWS, stride=nx), :]
            ebuf[at + i, pl.ds(zp * ROWS, ROWS), :] = line

    fetch_est.wait()
    for zp in range(zparts):
        turn(est.reshape(nz * nx, ny), nx, zp, 0, half)
    fetch_rec.wait()
    flat_z = zbuf.reshape(zbuf.shape[0] * nx, ny)
    for zp in range(zparts):
        rows = pl.ds(zp * ROWS, ROWS)
        for way, first, at in ((0, 0, half + nx), (1, nx - half, 0)):
            @pl.when(g_halo.has[1 - way])
            def _():
                e_copy(way, zp).wait_recv()
                turn(eland.at[way].reshape(nz * nx, ny), half, zp, first, at)

            @pl.when(jnp.logical_not(g_halo.has[1 - way]))
            def _():
                ebuf[at : at + half, rows, :] = jnp.zeros((half, ROWS, ny), ebuf.dtype)

        for xp in range(xparts):
            first = xp * GROUP
            for i, line in enumerate(blur(ebuf, wx, first, rows, False)):
                spot = (half + zp * ROWS) * nx + first + i
                flat_z[pl.ds(spot, ROWS, stride=nx), :] = y_forward(line, first + i, rows)
            z_halo.start(zp, xp)

    for xp in range(xparts):
        rows = pl.ds(xp * ROWS, ROWS)
        index = zi[0, rows, :] + 2 * profs
        for k in range(taps):
            wz[k, rows, :] = tap(k, index)

    reach = GROUP + taps - 1
    for xp in range(xparts):
        rows = pl.ds(xp * ROWS, ROWS)
        for zp in range(zparts):
            first = zp * GROUP
            z_halo.need(first, first + reach, xp)
            for i, blurred in enumerate(blur(zbuf, wz, first, rows, False)):
                rbuf[half + first + i, rows, :] = rec[0, first + i, rows, :] / blurred
            r_halo.start(zp, xp)

    flat_t = tbuf.reshape(nz * nx, ny)
    for zp in range(zparts):
        z_rows = pl.ds(zp * ROWS, ROWS)
        for xp in range(xparts):
            rows = pl.ds(xp * ROWS, ROWS)
            first = zp * GROUP
            r_halo.need(first, first + reach, xp)
            for i, line in enumerate(blur(rbuf, wz, first, rows, True)):
                tbuf[first + i, rows, :] = line

            def back_y(i, carry):
                x = xp * ROWS + i
                line = flat_t[pl.ds(zp * ROWS * nx + x, ROWS, stride=nx), :]
                gbuf[half + x, z_rows, :] = y_back(line, x, z_rows)
                return carry

            lax.fori_loop(0, ROWS, back_y, 0, unroll=4)
            g_halo.start(xp, zp)

    def view_copy(step, zp, xp):
        piece = vbuf.at[view, pl.ds(zp * ROWS, ROWS), pl.ds(xp * ROWS, ROWS)]
        slot = ((step - 1) * zparts + zp) * xparts + xp
        return pltpu.make_async_remote_copy(
            src_ref=piece, dst_ref=piece, send_sem=v_send.at[slot], recv_sem=v_recv.at[slot],
            device_id={"view": lax.rem(view + step, views)}, device_id_type=MESH,
        )

    flat_v = vbuf.reshape(views * nz * nx, ny)
    for zp in range(zparts):
        rows = pl.ds(zp * ROWS, ROWS)
        for xp in range(xparts):
            first = xp * GROUP
            g_halo.need(first, first + reach, zp)
            for i, line in enumerate(blur(gbuf, wx, first, rows, True)):
                flat_v[pl.ds((view * nz + zp * ROWS) * nx + first + i, ROWS, stride=nx), :] = line
            for step in range(1, views):
                view_copy(step, zp, xp).start()

    for halo in (z_halo, r_halo, g_halo):
        halo.finish()
    for way in (0, 1):
        @pl.when(g_halo.has[way])
        def _():
            for zp in range(zparts):
                e_copy(way, zp).wait_send()
    for zp in range(zparts):
        planes = pl.ds(zp * ROWS, ROWS)
        for xp in range(xparts):
            rows = pl.ds(xp * ROWS, ROWS)
            for step in range(1, views):
                view_copy(step, zp, xp).wait_recv()
            total = total_of(vbuf[v, planes, rows] for v in range(views))
            out[planes, rows] = est[planes, rows] * total / views
    for zp in range(zparts):
        for xp in range(xparts):
            for step in range(1, views):
                view_copy(step, zp, xp).wait_send()


def shards(sizes, *args):
    estimate, recorded, x_index, y_index, z_index, profiles = args
    views = sizes[0]
    nz, nx, ny = estimate.shape
    directions, profs, taps = profiles.shape[1:]
    assert recorded.shape[0] == 1
    half = taps // 2
    assert half <= min(nz, nx)
    assert directions * profs <= 128
    zparts, xparts = nz // ROWS, nx // ROWS
    f32 = jnp.float32
    counts = (zparts, *[zparts * xparts] * 3)
    sems = [pltpu.SemaphoreType.DMA((2 * c,)) for c in counts for _ in range(2)]
    sems += [pltpu.SemaphoreType.DMA((max(1, views - 1) * zparts * xparts,)) for _ in range(2)]
    return pl.pallas_call(
        functools.partial(kernel, sizes),
        out_shape=jax.ShapeDtypeStruct(estimate.shape, f32),
        in_specs=[pl.BlockSpec(memory_space=pltpu.HBM)] * 6,
        out_specs=pl.BlockSpec(memory_space=pltpu.VMEM),
        scratch_shapes=[
            *(pltpu.VMEM(a.shape, a.dtype) for a in args),
            pltpu.SemaphoreType.DMA((len(args),)),
            pltpu.VMEM((2, nz, nx, ny), f32),
            pltpu.VMEM((nx + 2 * half, nz, ny), f32),
            pltpu.VMEM((nz + 2 * half, nx, ny), f32),
            pltpu.VMEM((nz + 2 * half, nx, ny), f32),
            pltpu.VMEM((nx + 2 * half, nz, ny), f32),
            pltpu.VMEM((nz, nx, ny), f32),
            pltpu.VMEM((views, nz, nx, ny), f32),
            pltpu.VMEM((128, 128), f32),
            pltpu.VMEM((128, 128), f32),
            pltpu.VMEM((taps, nz, ny), f32),
            pltpu.VMEM((taps, nx, nz, ny), f32),
            pltpu.VMEM((taps, nx, ny), f32),
            *sems,
        ],
        compiler_params=pltpu.CompilerParams(
            collective_id=0, has_side_effects=True, vmem_limit_bytes=32 * 1024 * 1024
        ),
    )(*(pltpu.with_memory_space_constraint(a, pltpu.HBM) for a in args))


def solution(mesh):
    sizes = tuple(mesh.shape[name] for name in ("view", "tile", "slab"))
    placed = (
        P("slab", "tile", None),
        P("view", "slab", "tile", None),
        P("view", "slab", None),
        P("view", "slab", "tile"),
        P("view", "tile", None),
        P("view", None, None, None),
    )
    return jax.shard_map(
        functools.partial(shards, sizes),
        mesh=mesh, in_specs=placed, out_specs=P("slab", "tile", None), check_vma=False,
    )
```

```python
import functools

import jax
import jax.numpy as jnp
from jax import lax
from jax.experimental import pallas as pl
from jax.experimental.pallas import tpu as pltpu
from jax.sharding import PartitionSpec as P

MESH = pl.DeviceIdType.MESH
ROWS = 8
GROUP = ROWS


def total_of(terms):
    total = None
    for term in terms:
        total = term if total is None else total + term
    return total


def estimate_copy(halo, source, landing, sems, way, piece):
    planes = pl.ds(piece * ROWS, ROWS)
    slot = way * (source.shape[0] // ROWS) + piece
    return pltpu.make_async_remote_copy(
        src_ref=source.at[planes], dst_ref=landing.at[way, planes],
        send_sem=sems[0].at[slot], recv_sem=sems[1].at[slot],
        device_id={halo.axis: halo.to[way]}, device_id_type=MESH,
    )


class Halo:
    def __init__(self, buffer, axis, size, count, width, plane_pieces, row_pieces, rows, sems):
        self.buffer, self.axis, self.count, self.width = buffer, axis, count, width
        self.plane_pieces, self.row_pieces, self.rows = plane_pieces, row_pieces, rows
        self.send, self.recv = sems
        self.waited = set()
        here = lax.axis_index(axis)
        self.has = (here > 0, here < size - 1)
        self.to = (lax.max(here - 1, 0), lax.min(here + 1, size - 1))

    def planes(self, way, piece):
        length = self.count // self.plane_pieces
        low, high = piece * length, (piece + 1) * length
        if way == 0:
            high = min(high, self.width)
            return low, high, self.count + self.width + low
        low = max(low, self.count - self.width)
        return low, high, low - (self.count - self.width)

    def copy(self, way, piece, row_piece):
        low, high, landing = self.planes(way, piece)
        depth = self.rows // self.row_pieces
        rows = pl.ds(row_piece * depth, depth)
        slot = (way * self.plane_pieces + piece) * self.row_pieces + row_piece
        return pltpu.make_async_remote_copy(
            src_ref=self.buffer.at[pl.ds(self.width + low, high - low), rows],
            dst_ref=self.buffer.at[pl.ds(landing, high - low), rows],
            send_sem=self.send.at[slot],
            recv_sem=self.recv.at[slot],
            device_id={self.axis: self.to[way]},
            device_id_type=MESH,
        )

    def start(self, piece, row_piece):
        for way in (0, 1):
            @pl.when(self.has[way])
            def _():
                self.copy(way, piece, row_piece).start()

    def need(self, first, last, row_piece):
        for way in (0, 1):
            fresh = []
            for piece in range(self.plane_pieces):
                low, high, landing = self.planes(way, piece)
                spot = (way, piece, row_piece)
                if landing < last and landing + high - low > first and spot not in self.waited:
                    self.waited.add(spot)
                    fresh.append(piece)
            if fresh:
                @pl.when(self.has[1 - way])
                def _():
                    for piece in fresh:
                        self.copy(way, piece, row_piece).wait_recv()

    def finish(self):
        for way in (0, 1):
            @pl.when(self.has[way])
            def _():
                for piece in range(self.plane_pieces):
                    for row_piece in range(self.row_pieces):
                        self.copy(way, piece, row_piece).wait_send()

    def clear_ends(self):
        blank = jnp.zeros((self.width,) + self.buffer.shape[1:], self.buffer.dtype)

        @pl.when(jnp.logical_not(self.has[0]))
        def _():
            self.buffer[: self.width] = blank

        @pl.when(jnp.logical_not(self.has[1]))
        def _():
            self.buffer[self.count + self.width : self.count + 2 * self.width] = blank


def kernel(
    sizes, est_hbm, rec_hbm, xi_hbm, yi_hbm, zi_hbm, prof_hbm, out,
    est, rec, xi, yi, zi, prof, in_sems, eland, ebuf, zbuf, rbuf, gbuf, tbuf, vbuf, table_in, table, wx, wy, wz,
    e_send, e_recv, z_send, z_recv, r_send, r_recv, g_send, g_recv, v_send, v_recv,
):
    views, tiles, slabs = sizes
    sources = (est_hbm, prof_hbm, xi_hbm, yi_hbm, zi_hbm, rec_hbm)
    fetches = [
        pltpu.make_async_copy(source, target, in_sems.at[i])
        for i, (source, target) in enumerate(zip(sources, (est, prof, xi, yi, zi, rec)))
    ]
    fetch_est, *fetch_taps, fetch_rec = fetches
    nz, nx, ny = est.shape
    directions, profs, taps = prof.shape[1:]
    half = taps // 2
    zparts, xparts = nz // ROWS, nx // ROWS
    z_halo = Halo(zbuf, "slab", slabs, nz, half, zparts, xparts, nx, (z_send, z_recv))
    r_halo = Halo(rbuf, "slab", slabs, nz, half, zparts, xparts, nx, (r_send, r_recv))
    g_halo = Halo(gbuf, "tile", tiles, nx, half, xparts, zparts, nz, (g_send, g_recv))
    view = lax.axis_index("view")

    barrier = pltpu.get_barrier_semaphore()
    heard = views - 1
    for halo in (g_halo, z_halo):
        for way in (0, 1):
            heard = heard + halo.has[way].astype(jnp.int32)

            @pl.when(halo.has[way])
            def _():
                pl.semaphore_signal(barrier, inc=1, device_id={halo.axis: halo.to[way]}, device_id_type=MESH)
    for step in range(1, views):
        pl.semaphore_signal(
            barrier, inc=1, device_id={"view": lax.rem(view + step, views)}, device_id_type=MESH
        )

    for fetch in fetch_taps:
        fetch.start()
    pl.semaphore_wait(barrier, heard)
    e_copy = functools.partial(estimate_copy, g_halo, est_hbm, eland, (e_send, e_recv))
    for zp in range(zparts):
        for way in (0, 1):
            @pl.when(g_halo.has[way])
            def _():
                e_copy(way, zp).start()

    fetch_est.start()
    fetch_rec.start()

    for halo in (z_halo, r_halo, g_halo):
        halo.clear_ends()
    for fetch in fetch_taps:
        fetch.wait()
    table_in[...] = jnp.zeros(table_in.shape, table_in.dtype)
    for a in range(directions):
        profile = prof[0, a]
        table_in[pl.ds(a * profs, profs), pl.ds(0, taps)] = profile / jnp.sum(profile, axis=-1, keepdims=True)
    table[...] = table_in[...].T

    steps = int(taps**0.5) + 1

    def coarse_of(k):
        return (k - half) // steps * steps

    def y_forward(line, x, rows):
        shifted, partial = {}, {}
        for k in range(taps):
            coarse = coarse_of(k)
            fine = k - half - coarse
            if fine not in shifted:
                shifted[fine] = pltpu.roll(line, -fine % ny, 1) if fine else line
            term = wy[k, x, rows, :] * shifted[fine]
            partial[coarse] = partial[coarse] + term if coarse in partial else term
        return total_of(pltpu.roll(v, -c % ny, 1) if c else v for c, v in partial.items())

    def y_back(line, x, rows):
        shifted, partial = {}, {}
        for k in range(taps):
            coarse = coarse_of(k)
            fine = k - half - coarse
            if coarse not in shifted:
                shifted[coarse] = pltpu.roll(line, coarse % ny, 1) if coarse else line
            term = wy[k, x, rows, :] * shifted[coarse]
            partial[fine] = partial[fine] + term if fine in partial else term
        return total_of(pltpu.roll(v, f, 1) if f else v for f, v in partial.items())

    def tap(k, index):
        row = jnp.broadcast_to(table[pl.ds(k, 1), :], (ROWS, table.shape[1]))
        return jnp.take_along_axis(row, index, axis=1, mode="promise_in_bounds")

    for zp in range(zparts):
        rows = pl.ds(zp * ROWS, ROWS)
        index = xi[0, rows, :]
        for k in range(taps):
            wx[k, rows, :] = tap(k, index)
    lane = lax.broadcasted_iota(jnp.int32, (ROWS, ny), 1)
    inside = []
    for k in range(taps):
        read = lax.rem(lane + (ny - coarse_of(k)), ny) + (k - half)
        inside.append((read >= 0) & (read < ny))
    for zp in range(zparts):
        rows = pl.ds(zp * ROWS, ROWS)
        lines = yi[0, rows, :]
        for x in range(nx):
            index = jnp.broadcast_to(lines[:, x : x + 1], (ROWS, ny)) + profs
            for k in range(taps):
                wy[k, x, rows, :] = jnp.where(inside[k], tap(k, index), 0.0)
    def blur(field, weights, first, rows, adjoint):
        totals, loaded = [None] * GROUP, {}
        for j in range(GROUP + taps - 1):
            read = field[first + j, rows, :]
            for i in range(max(0, j - taps + 1), min(GROUP, j + 1)):
                k = taps - 1 - (j - i) if adjoint else j - i
                if k not in loaded:
                    loaded[k] = weights[k, rows, :]
                term = loaded[k] * read
                totals[i] = term if totals[i] is None else totals[i] + term
        return totals

    def turn(source, planes, zp, first, at):
        for i in range(planes):
            line = source[pl.ds(zp * ROWS * nx + first + i, ROWS, stride=nx), :]
            ebuf[at + i, pl.ds(zp * ROWS, ROWS), :] = line

    fetch_est.wait()
    for zp in range(zparts):
        turn(est.reshape(nz * nx, ny), nx, zp, 0, half)
    fetch_rec.wait()
    flat_z = zbuf.reshape(zbuf.shape[0] * nx, ny)
    for zp in range(zparts):
        rows = pl.ds(zp * ROWS, ROWS)
        for way, first, at in ((0, 0, half + nx), (1, nx - half, 0)):
            @pl.when(g_halo.has[1 - way])
            def _():
                e_copy(way, zp).wait_recv()
                turn(eland.at[way].reshape(nz * nx, ny), half, zp, first, at)

            @pl.when(jnp.logical_not(g_halo.has[1 - way]))
            def _():
                ebuf[at : at + half, rows, :] = jnp.zeros((half, ROWS, ny), ebuf.dtype)

        for xp in range(xparts):
            first = xp * GROUP
            for i, line in enumerate(blur(ebuf, wx, first, rows, False)):
                spot = (half + zp * ROWS) * nx + first + i
                flat_z[pl.ds(spot, ROWS, stride=nx), :] = y_forward(line, first + i, rows)
            z_halo.start(zp, xp)

    for xp in range(xparts):
        rows = pl.ds(xp * ROWS, ROWS)
        index = zi[0, rows, :] + 2 * profs
        for k in range(taps):
            wz[k, rows, :] = tap(k, index)

    reach = GROUP + taps - 1
    for xp in range(xparts):
        rows = pl.ds(xp * ROWS, ROWS)
        for zp in range(zparts):
            first = zp * GROUP
            z_halo.need(first, first + reach, xp)
            for i, blurred in enumerate(blur(zbuf, wz, first, rows, False)):
                rbuf[half + first + i, rows, :] = rec[0, first + i, rows, :] / blurred
            r_halo.start(zp, xp)

    flat_t = tbuf.reshape(nz * nx, ny)
    for zp in range(zparts):
        z_rows = pl.ds(zp * ROWS, ROWS)
        for xp in range(xparts):
            rows = pl.ds(xp * ROWS, ROWS)
            first = zp * GROUP
            r_halo.need(first, first + reach, xp)
            for i, line in enumerate(blur(rbuf, wz, first, rows, True)):
                tbuf[first + i, rows, :] = line

            for x in range(xp * ROWS, (xp + 1) * ROWS):
                line = flat_t[pl.ds(zp * ROWS * nx + x, ROWS, stride=nx), :]
                gbuf[half + x, z_rows, :] = y_back(line, x, z_rows)
            g_halo.start(xp, zp)

    def view_copy(step, zp, xp):
        piece = vbuf.at[view, pl.ds(zp * ROWS, ROWS), pl.ds(xp * ROWS, ROWS)]
        slot = ((step - 1) * zparts + zp) * xparts + xp
        return pltpu.make_async_remote_copy(
            src_ref=piece, dst_ref=piece, send_sem=v_send.at[slot], recv_sem=v_recv.at[slot],
            device_id={"view": lax.rem(view + step, views)}, device_id_type=MESH,
        )

    flat_v = vbuf.reshape(views * nz * nx, ny)
    for zp in range(zparts):
        rows = pl.ds(zp * ROWS, ROWS)
        for xp in range(xparts):
            first = xp * GROUP
            g_halo.need(first, first + reach, zp)
            for i, line in enumerate(blur(gbuf, wx, first, rows, True)):
                flat_v[pl.ds((view * nz + zp * ROWS) * nx + first + i, ROWS, stride=nx), :] = line
            for step in range(1, views):
                view_copy(step, zp, xp).start()

    for halo in (z_halo, r_halo, g_halo):
        halo.finish()
    for way in (0, 1):
        @pl.when(g_halo.has[way])
        def _():
            for zp in range(zparts):
                e_copy(way, zp).wait_send()
    for zp in range(zparts):
        planes = pl.ds(zp * ROWS, ROWS)
        for xp in range(xparts):
            rows = pl.ds(xp * ROWS, ROWS)
            for step in range(1, views):
                view_copy(step, zp, xp).wait_recv()
            total = total_of(vbuf[v, planes, rows] for v in range(views))
            out[planes, rows] = est[planes, rows] * total / views
    for zp in range(zparts):
        for xp in range(xparts):
            for step in range(1, views):
                view_copy(step, zp, xp).wait_send()


def shards(sizes, *args):
    estimate, recorded, x_index, y_index, z_index, profiles = args
    views = sizes[0]
    nz, nx, ny = estimate.shape
    directions, profs, taps = profiles.shape[1:]
    assert recorded.shape[0] == 1
    half = taps // 2
    assert half <= min(nz, nx)
    assert directions * profs <= 128
    zparts, xparts = nz // ROWS, nx // ROWS
    f32 = jnp.float32
    counts = (zparts, *[zparts * xparts] * 3)
    sems = [pltpu.SemaphoreType.DMA((2 * c,)) for c in counts for _ in range(2)]
    sems += [pltpu.SemaphoreType.DMA((max(1, views - 1) * zparts * xparts,)) for _ in range(2)]
    return pl.pallas_call(
        functools.partial(kernel, sizes),
        out_shape=jax.ShapeDtypeStruct(estimate.shape, f32),
        in_specs=[pl.BlockSpec(memory_space=pltpu.HBM)] * 6,
        out_specs=pl.BlockSpec(memory_space=pltpu.VMEM),
        scratch_shapes=[
            *(pltpu.VMEM(a.shape, a.dtype) for a in args),
            pltpu.SemaphoreType.DMA((len(args),)),
            pltpu.VMEM((2, nz, nx, ny), f32),
            pltpu.VMEM((nx + 2 * half, nz, ny), f32),
            pltpu.VMEM((nz + 2 * half, nx, ny), f32),
            pltpu.VMEM((nz + 2 * half, nx, ny), f32),
            pltpu.VMEM((nx + 2 * half, nz, ny), f32),
            pltpu.VMEM((nz, nx, ny), f32),
            pltpu.VMEM((views, nz, nx, ny), f32),
            pltpu.VMEM((128, 128), f32),
            pltpu.VMEM((128, 128), f32),
            pltpu.VMEM((taps, nz, ny), f32),
            pltpu.VMEM((taps, nx, nz, ny), f32),
            pltpu.VMEM((taps, nx, ny), f32),
            *sems,
        ],
        compiler_params=pltpu.CompilerParams(
            collective_id=0, has_side_effects=True, vmem_limit_bytes=32 * 1024 * 1024
        ),
    )(*(pltpu.with_memory_space_constraint(a, pltpu.HBM) for a in args))


def solution(mesh):
    sizes = tuple(mesh.shape[name] for name in ("view", "tile", "slab"))
    placed = (
        P("slab", "tile", None),
        P("view", "slab", "tile", None),
        P("view", "slab", None),
        P("view", "slab", "tile"),
        P("view", "tile", None),
        P("view", None, None, None),
    )
    return jax.shard_map(
        functools.partial(shards, sizes),
        mesh=mesh, in_specs=placed, out_specs=P("slab", "tile", None), check_vma=False,
    )
```
